512 devices in a mesh: wide: 64 (over x, z), narrow: 8 (over y, core).
Axes of the slice: x: 4, y: 4, z: 16, core: 2. Of those that a mesh axis runs over, the one named last changes fastest.
Arguments:
- amplitudes: bfloat16 [2048, 8192], P(('wide', 'narrow')), may hold values from -6 to 6
- amp_mask: int32 [32, 128], replicated, may hold values from 0 to 1, as said below
- integrals: bfloat16 [2048, 32768], P('narrow', 'wide'), may hold values from -0.59765625 to 0.59765625
- int_mask: int32 [32, 512], replicated, may hold values from 0 to 1, as said below
- owner: int32 [512], replicated, may hold values from 0 to 511, each once
- occ_energy: float32 [8192], P('narrow'), may hold values from -3 to -0.5
- vir_energy: float32 [32768], replicated, may hold values from 1 to 8
Outputs:
- update: bfloat16 [8192, 32768], P('narrow', 'wide')
The draws below stay inside these ranges and needn't reach their ends.
Inputs may be any that keep to these rules, and one draw needn't show every extreme that they name: `amp_mask`: 1 marks a pair of tiles within the screening distance, 0 one outside it. `int_mask`: 1 marks a pair of tiles within the screening distance, 0 one outside it. A permutation of the 512 tiles; columns 64 * s to 64 * s + 63 of integrals and update belong to tile owner[s].
All inputs are finite; a program needn't handle non-finite values.
Results may differ from the reference program's by a relative error of at most 0.001.
Values may be sent and summed in bfloat16 or wider, within the bound.
No kernel may reach another device: no remote copies, remote signals or barrier semaphores. Data moves between devices by JAX's collectives and lax.ppermute only.
A program may use at most 64 MiB of HBM per device.

```python
import jax
import jax.numpy as jnp
from jax import lax

TILE = 64
K_TILES = 32
Q_DEV = 512
K = 2048
OP = 8192
Q = 32768
OP_TILES = 128
Q_TILES = 512
N_WIDE = 64


span_units = 1024


reach_units = 256


def tile_positions(key):
    vir_pos = jax.random.randint(jax.random.fold_in(key, 11), (K_TILES,), 0, span_units)
    occ_base = jnp.arange(OP_TILES, dtype=jnp.int32) * span_units // OP_TILES
    occ_pos = occ_base + jax.random.randint(jax.random.fold_in(key, 12), (OP_TILES,), 0, max(span_units // OP_TILES, 1))
    out_pos = jax.random.randint(jax.random.fold_in(key, 13), (Q_TILES,), 0, span_units)
    return (vir_pos, occ_pos, out_pos)


def draw_amp_mask(key, part):
    vir_pos, occ_pos, out_pos = tile_positions(key)
    return jnp.where(jnp.abs(vir_pos[:, None] - occ_pos[None, :]) <= reach_units, 1, 0).astype(jnp.int32)


def draw_int_mask(key, part):
    vir_pos, occ_pos, out_pos = tile_positions(key)
    return jnp.where(jnp.abs(vir_pos[:, None] - out_pos[None, :]) <= reach_units, 1, 0).astype(jnp.int32)


def shard_levels(stream_key, shape, shards, low, top_value):
    factor_of, own = 1.0, jax.random.fold_in(stream_key, 6)
    for position, parts in shards:
        heights = jnp.exp(jax.random.uniform(jax.random.fold_in(own, position), (parts,), jnp.float32, low / len(shards), top_value / len(shards)))
        factor_of = factor_of * jnp.repeat(heights, shape[position] // parts).reshape([-1 if axis == position else 1 for axis in range(len(shape))])
    return factor_of


def bell_draw(own_key, extent, spread, most, pieces=(), kind=jnp.bfloat16):
    values = jax.random.normal(own_key, extent, jnp.float32) * spread
    if len(pieces) > 0:
        values = shard_levels(own_key, extent, pieces, -0.22, 0.18) * values
    return jnp.clip(values, min=-most, max=most).astype(kind)


def setup_inputs(seed: int = 0) -> dict:
    key_of = jax.random.split(jax.random.key(seed), 8)
    return {
        "amplitudes": bell_draw(key_of[0], (K, OP), 1.0, 6.0, ((0, 512),)),
        "amp_mask": draw_amp_mask(jax.random.fold_in(key_of[7], 71), 0),
        "integrals": bell_draw(key_of[2], (K, Q), 0.1, 0.59765625, ((0, 8), (1, 64))),
        "int_mask": draw_int_mask(jax.random.fold_in(key_of[7], 71), 0),
        "owner": jax.random.permutation(key_of[4], Q_TILES).astype(jnp.int32),
        "occ_energy": jnp.clip(-3.0 + 2.5 * jax.random.uniform(key_of[5], (OP,), jnp.float32) ** shard_levels(key_of[5], (OP,), ((0, 8),), -0.2, 0.2), -3.0, -0.5),
        "vir_energy": jnp.clip(jax.random.uniform(key_of[6], (Q,), jnp.float32, 1.0, 8.0), 1.0, 8.0),
    }


def reference(amplitudes, amp_mask, integrals, int_mask, owner, occ_energy, vir_energy):
    amp_wide = jnp.repeat(jnp.repeat(amp_mask, TILE, axis=0), TILE, axis=1)
    masked = jnp.where(amp_wide == 1, amplitudes, jnp.zeros((), amplitudes.dtype))
    amp_trans = masked.T
    per_block = Q_DEV // TILE
    vir_tiles = vir_energy.reshape(Q_TILES, TILE)

    def one_block(block_index):
        slot_ids = block_index * per_block + jnp.arange(per_block, dtype=jnp.int32)
        tile_ids = owner[slot_ids]
        col_mask = jnp.repeat(jnp.repeat(int_mask[:, tile_ids], TILE, axis=0), TILE, axis=1)
        int_panel = lax.dynamic_slice_in_dim(integrals, (block_index * Q_DEV).astype(jnp.int32), Q_DEV, 1)
        int_panel = jnp.where(col_mask == 1, int_panel, jnp.zeros((), integrals.dtype))
        ladder = jnp.dot(amp_trans, int_panel, preferred_element_type=jnp.float32)
        energy = vir_tiles[tile_ids].reshape(Q_DEV)
        denominator = energy[None, :] - occ_energy[:, None]
        return (ladder / denominator).astype(jnp.bfloat16)

    blocks = lax.map(one_block, jnp.arange(N_WIDE, dtype=jnp.int32))
    return blocks.transpose(1, 0, 2).reshape(OP, Q)
```

```python
import jax
import jax.numpy as jnp
from jax import lax
from jax.experimental import pallas as pl
from jax.experimental.pallas import tpu as pltpu
from jax.sharding import PartitionSpec as P

TILE = 64
NX, NZ, NY = 4, 16, 4
NZC, NZF = 4, 4
SPLIT = 512


def from_z(value, offset):
    pairs = [(x * NZ + (z + offset) % NZ, x * NZ + z) for x in range(NX) for z in range(NZ)]
    return lax.ppermute(value, "wide", pairs)


def from_y(value, offset):
    pairs = [(((y + offset) % NY) * 2 + c, y * 2 + c) for y in range(NY) for c in range(2)]
    return lax.ppermute(value, "narrow", pairs)


def from_partner(value):
    return lax.ppermute(value, "narrow", [(n ^ 1, n) for n in range(2 * NY)])


def share(value, groups):
    copies = jnp.broadcast_to(value[None], (len(groups[0]),) + value.shape)
    return lax.all_to_all(
        copies, "wide", split_axis=0, concat_axis=0, axis_index_groups=groups, tiled=True
    )


ALONG_X = [[x * NZ + z for x in range(NX)] for z in range(NZ)]
COARSE_Z = [[x * NZ + c * NZF + f for c in range(NZC)] for x in range(NX) for f in range(NZF)]


def ladder_kernel(
    first_ref, s0, s1, s2, s3, s4, own_int, other_int, vir_ref, occ_ref, out_ref,
    amp, ints, amp_sems, int_sems,
):
    step = pl.program_id(0)
    wide = lax.axis_index("wide")
    narrow = lax.axis_index("narrow")
    z = lax.rem(wide, NZ)
    y, core = lax.div(narrow, 2), lax.rem(narrow, 2)
    rows = amp.shape[3]

    def fine(offset):
        return lax.rem(lax.rem(z + offset + NZ, NZ), NZF)

    early, late = [], []
    count = 0
    for x in range(NX):
        for slot, offset in enumerate((0, 1, -1, 2)):
            early.append(
                pltpu.make_async_copy(
                    first_ref.at[x, slot],
                    amp.at[x, :, fine(offset), :, pl.ds(0, SPLIT)],
                    amp_sems.at[count],
                )
            )
            count += 1
    for piece, offset, lo, n in (
        (s0, 0, 0, NZC), (s1, 1, 0, NZC), (s2, -1, 0, NZC), (s3, 2, 0, 2), (s4, -2, 2, 2),
    ):
        for x in range(NX):
            late.append(
                pltpu.make_async_copy(
                    piece.at[x],
                    amp.at[x, pl.ds(lo, n), fine(offset), :, pl.ds(SPLIT, amp.shape[4] - SPLIT)],
                    amp_sems.at[count],
                )
            )
            count += 1
    int_copies = []
    for slot, offset in enumerate((0, 1, -1, 2)):
        there = lax.rem(y + offset + NY, NY)
        for place, (ref, c) in enumerate(((own_int, core), (other_int, 1 - core))):
            int_copies.append(
                pltpu.make_async_copy(
                    ref.at[slot], ints.at[there, c], int_sems.at[2 * slot + place]
                )
            )

    @pl.when(step == 0)
    def _():
        for copy in int_copies + early + late:
            copy.start()
        for copy in int_copies + early + late:
            copy.wait()

    width = out_ref.shape[0]
    at = pl.multiple_of(step * width, width)
    k_total = NX * NZ * rows
    part = amp[:, :, :, :, pl.ds(at, width)].reshape(k_total, width)
    whole = ints[...].reshape(k_total, ints.shape[3])
    ladder = lax.dot_general(
        part, whole, (((0,), (0,)), ((), ())), preferred_element_type=jnp.float32
    )
    out_ref[...] = (ladder / (vir_ref[...] - occ_ref[...])).astype(out_ref.dtype)


def shards(amplitudes, amp_mask, integrals, int_mask, owner, occ_energy, vir_energy):
    wide = lax.axis_index("wide")
    narrow = lax.axis_index("narrow")
    src_rows, occ_all = amplitudes.shape
    occ_here = occ_energy.shape[0]
    int_rows, vir_here = integrals.shape
    narrow_count = lax.axis_size("narrow")
    rows = src_rows * narrow_count

    first_src = (wide * narrow_count + narrow) * src_rows
    amp_row = lax.dynamic_slice_in_dim(amp_mask, first_src // TILE, 1, 0)
    amp_wide = jnp.broadcast_to(
        amp_row[:, :, None], (src_rows, occ_all // TILE, TILE)
    ).reshape(src_rows, occ_all)
    masked = jnp.where(amp_wide == 1, amplitudes, jnp.zeros((), amplitudes.dtype))

    vir_tiles_here = vir_here // TILE
    tile_ids = lax.dynamic_slice_in_dim(owner, wide * vir_tiles_here, vir_tiles_here, 0)
    row_tiles = int_rows // TILE
    int_mask_rows = lax.dynamic_slice_in_dim(int_mask, narrow * row_tiles, row_tiles, 0)
    local_mask = jnp.take(int_mask_rows, tile_ids, axis=1)
    local_wide = jnp.broadcast_to(
        local_mask[:, None, :, None], (row_tiles, TILE, vir_tiles_here, TILE)
    ).reshape(int_rows, vir_here)
    int_masked = jnp.where(local_wide == 1, integrals, jnp.zeros((), integrals.dtype))
    masked, int_masked = lax.optimization_barrier((masked, int_masked))

    block = lax.all_to_all(
        masked.reshape(src_rows, narrow_count, occ_here),
        "narrow", split_axis=1, concat_axis=0, tiled=True,
    ).reshape(rows, occ_here)

    coarse = share(block, COARSE_Z).reshape(NZC, rows, occ_here)
    own_int = jnp.stack(
        [int_masked, from_y(int_masked, 1), from_y(int_masked, -1), from_y(int_masked, 2)]
    )
    coarse, own_int = lax.optimization_barrier((coarse, own_int))
    other_int = from_partner(own_int)

    part_a, part_c = coarse[:, :, :SPLIT], coarse[:, :, SPLIT:]
    fine_a = jnp.stack([part_a, from_z(part_a, 2), from_z(part_a, 1), from_z(part_a, -1)])
    fine_a = jnp.stack([fine_a[0], fine_a[2], fine_a[3], fine_a[1]])
    x_c = share(part_c, ALONG_X).reshape((NX,) + part_c.shape)
    half = NZC // 2
    x_c, fine_a, other_int = lax.optimization_barrier((x_c, fine_a, other_int))
    whole_a = share(fine_a, ALONG_X).reshape((NX,) + fine_a.shape)
    c2 = from_z(x_c[:, :half], 2)
    c3 = from_z(x_c[:, half:], -2)
    c0 = from_z(x_c, 1)
    c1 = from_z(x_c, -1)

    vir_here_energy = jnp.take(vir_energy.reshape(-1, TILE), tile_ids, axis=0).reshape(1, vir_here)
    steps = 4
    width = occ_here // steps
    any_spec = pl.BlockSpec(memory_space=pl.ANY)
    k_total = NX * NZ * rows
    return pl.pallas_call(
        ladder_kernel,
        grid=(steps,),
        in_specs=[any_spec] * 8
        + [
            pl.BlockSpec((1, vir_here), lambda i: (0, 0)),
            pl.BlockSpec((width, 1), lambda i: (i, 0)),
        ],
        out_specs=pl.BlockSpec((width, vir_here), lambda i: (i, 0)),
        out_shape=jax.ShapeDtypeStruct((occ_here, vir_here), jnp.bfloat16),
        scratch_shapes=[
            pltpu.VMEM((NX, NZC, NZF, rows, occ_here), jnp.bfloat16),
            pltpu.VMEM((NY, 2, int_rows, vir_here), jnp.bfloat16),
            pltpu.SemaphoreType.DMA((36,)),
            pltpu.SemaphoreType.DMA((8,)),
        ],
        compiler_params=pltpu.CompilerParams(vmem_limit_bytes=40 * 2**20),
        cost_estimate=pl.CostEstimate(
            flops=2 * occ_here * vir_here * k_total, bytes_accessed=8 * 2**20, transcendentals=0
        ),
        name="ladder",
    )(
        whole_a, x_c, c0, c1, c2, c3, own_int, other_int,
        vir_here_energy, occ_energy.reshape(occ_here, 1),
    )


def solution(mesh):
    return jax.shard_map(
        shards,
        mesh=mesh,
        in_specs=(
            P(("wide", "narrow"), None),
            P(),
            P("narrow", "wide"),
            P(),
            P(),
            P("narrow"),
            P(),
        ),
        out_specs=P("narrow", "wide"),
        check_vma=False,
    )
```

```python
import jax
import jax.numpy as jnp
from jax import lax
from jax.experimental import pallas as pl
from jax.experimental.pallas import tpu as pltpu
from jax.sharding import PartitionSpec as P

TILE = 64
NX, NZ = 4, 16
NZC, NZF = 4, 4
SPLIT = 640


def from_z(value, offset):
    pairs = [(x * NZ + (z + offset) % NZ, x * NZ + z) for x in range(NX) for z in range(NZ)]
    return lax.ppermute(value, "wide", pairs)


def from_x(value, offset):
    pairs = [(((x + offset) % NX) * NZ + z, x * NZ + z) for x in range(NX) for z in range(NZ)]
    return lax.ppermute(value, "wide", pairs)


def share(value, groups):
    return lax.all_gather(value, "wide", axis_index_groups=groups)


ALONG_X = [[x * NZ + z for x in range(NX)] for z in range(NZ)]
COARSE_Z = [[x * NZ + c * NZF + f for c in range(NZC)] for x in range(NX) for f in range(NZF)]


def ladder_kernel(
    a0, a1, a2, a3, s0, s1, s2, s3, int_ref, vir_ref, occ_ref, out_ref, amp, ints, sems
):
    step = pl.program_id(0)
    wide = lax.axis_index("wide")
    z, x = lax.rem(wide, NZ), lax.div(wide, NZ)
    rows = amp.shape[3]

    def place(there_x, z_offset, at, width):
        there_z = lax.rem(z + z_offset + NZ, NZ)
        return amp.at[there_x, :, lax.rem(there_z, NZF), :, pl.ds(at, width)]

    moves = [(int_ref, ints)]
    for slot, z_offset in enumerate((0, 1, -1, 2)):
        for ref, x_offset in ((a0, 0), (a1, 1), (a2, -1), (a3, 2)):
            there_x = lax.rem(x + x_offset + NX, NX)
            moves.append((ref.at[slot], place(there_x, z_offset, 0, SPLIT)))
        for n in range(NX):
            ref = (s0, s1, s2, s3)[slot]
            moves.append((ref.at[n], place(n, z_offset, SPLIT, amp.shape[4] - SPLIT)))
    copies = [pltpu.make_async_copy(a, b, sems.at[n]) for n, (a, b) in enumerate(moves)]

    @pl.when(step == 0)
    def _():
        for copy in copies:
            copy.start()
        for copy in copies:
            copy.wait()

    width = out_ref.shape[0]
    at = pl.multiple_of(step * width, width)
    k_total = NX * NZ * rows
    part = amp[:, :, :, :, pl.ds(at, width)].reshape(k_total, width)
    ladder = lax.dot_general(
        part, ints[...], (((0,), (0,)), ((), ())), preferred_element_type=jnp.float32
    )
    out_ref[...] = (ladder / (vir_ref[...] - occ_ref[...])).astype(out_ref.dtype)


def shards(amplitudes, amp_mask, integrals, int_mask, owner, occ_energy, vir_energy):
    wide = lax.axis_index("wide")
    narrow = lax.axis_index("narrow")
    src_rows, occ_all = amplitudes.shape
    occ_here = occ_energy.shape[0]
    int_rows, vir_here = integrals.shape
    narrow_count = lax.axis_size("narrow")
    rows = src_rows * narrow_count

    first_src = (wide * narrow_count + narrow) * src_rows
    amp_row = lax.dynamic_slice_in_dim(amp_mask, first_src // TILE, 1, 0)
    amp_wide = jnp.broadcast_to(
        amp_row[:, :, None], (src_rows, occ_all // TILE, TILE)
    ).reshape(src_rows, occ_all)
    masked = jnp.where(amp_wide == 1, amplitudes, jnp.zeros((), amplitudes.dtype))

    block = lax.all_to_all(
        masked.reshape(src_rows, narrow_count, occ_here),
        "narrow", split_axis=1, concat_axis=0, tiled=True,
    ).reshape(rows, occ_here)
    block, integrals = lax.optimization_barrier((block, integrals))
    coarse = share(block, COARSE_Z)

    vir_tiles_here = vir_here // TILE
    tile_ids = lax.dynamic_slice_in_dim(owner, wide * vir_tiles_here, vir_tiles_here, 0)
    row_tiles = int_rows // TILE
    int_mask_rows = lax.dynamic_slice_in_dim(int_mask, narrow * row_tiles, row_tiles, 0)
    local_mask = jnp.take(int_mask_rows, tile_ids, axis=1)
    local_wide = jnp.broadcast_to(
        local_mask[:, None, :, None], (row_tiles, TILE, vir_tiles_here, TILE)
    ).reshape(int_rows, vir_here)
    int_masked = jnp.where(local_wide == 1, integrals, jnp.zeros((), integrals.dtype))
    int_copies = jnp.broadcast_to(int_masked[None], (narrow_count,) + int_masked.shape)
    int_full = lax.all_to_all(
        int_copies, "narrow", split_axis=0, concat_axis=0, tiled=True
    ).reshape(int_rows * narrow_count, vir_here)

    part_a, part_c = coarse[:, :, :SPLIT], coarse[:, :, SPLIT:]
    fine_a = [from_z(part_a, 2), from_z(part_a, 1), from_z(part_a, -1)]
    x_c = share(part_c, ALONG_X)
    fine_a = jnp.stack([part_a, fine_a[1], fine_a[2], fine_a[0]])
    x_c, fine_a = lax.optimization_barrier((x_c, fine_a))
    a3 = from_x(fine_a, 2)
    a1, a2 = from_x(fine_a, 1), from_x(fine_a, -1)
    c2 = from_z(x_c, 2)
    c0 = from_z(x_c, 1)
    c1 = from_z(x_c, -1)

    vir_here_energy = jnp.take(vir_energy.reshape(-1, TILE), tile_ids, axis=0).reshape(1, vir_here)
    steps = 4
    width = occ_here // steps
    any_spec = pl.BlockSpec(memory_space=pl.ANY)
    k_total = NX * NZ * rows
    return pl.pallas_call(
        ladder_kernel,
        grid=(steps,),
        in_specs=[any_spec] * 9
        + [
            pl.BlockSpec((1, vir_here), lambda i: (0, 0)),
            pl.BlockSpec((width, 1), lambda i: (i, 0)),
        ],
        out_specs=pl.BlockSpec((width, vir_here), lambda i: (i, 0)),
        out_shape=jax.ShapeDtypeStruct((occ_here, vir_here), jnp.bfloat16),
        scratch_shapes=[
            pltpu.VMEM((NX, NZC, NZF, rows, occ_here), jnp.bfloat16),
            pltpu.VMEM((k_total, vir_here), jnp.bfloat16),
            pltpu.SemaphoreType.DMA((1 + 2 * NX * NZF,)),
        ],
        compiler_params=pltpu.CompilerParams(vmem_limit_bytes=40 * 2**20),
        cost_estimate=pl.CostEstimate(
            flops=2 * occ_here * vir_here * k_total, bytes_accessed=8 * 2**20, transcendentals=0
        ),
        name="ladder",
    )(
        fine_a, a1, a2, a3, x_c, c0, c1, c2, int_full,
        vir_here_energy, occ_energy.reshape(occ_here, 1),
    )


def solution(mesh):
    return jax.shard_map(
        shards,
        mesh=mesh,
        in_specs=(
            P(("wide", "narrow"), None),
            P(),
            P("narrow", "wide"),
            P(),
            P(),
            P("narrow"),
            P(),
        ),
        out_specs=P("narrow", "wide"),
        check_vma=False,
    )
```

```python
import jax
import jax.numpy as jnp
from jax import lax
from jax.experimental import pallas as pl
from jax.experimental.pallas import tpu as pltpu
from jax.sharding import PartitionSpec as P

TILE = 64
NX, NZ = 4, 16
NZC, NZF = 4, 4
SPLIT = 640


def from_z(value, offset):
    pairs = [(x * NZ + (z + offset) % NZ, x * NZ + z) for x in range(NX) for z in range(NZ)]
    return lax.ppermute(value, "wide", pairs)


def from_x(value, offset):
    pairs = [(((x + offset) % NX) * NZ + z, x * NZ + z) for x in range(NX) for z in range(NZ)]
    return lax.ppermute(value, "wide", pairs)


def share(value, groups):
    return lax.all_gather(value, "wide", axis_index_groups=groups)


ALONG_X = [[x * NZ + z for x in range(NX)] for z in range(NZ)]
COARSE_Z = [[x * NZ + c * NZF + f for c in range(NZC)] for x in range(NX) for f in range(NZF)]


def ladder_kernel(moves_of, lo, refs, scratch):
    pieces, (int_ref, vir_ref, occ_ref), out_ref = refs
    amp, ints, result, sems, out_sem = scratch
    rows, width = amp.shape[3:]
    wide = lax.axis_index("wide")
    moves = [(int_ref, ints)] + moves_of(pieces, amp, lax.div(wide, NZ), lax.rem(wide, NZ))
    copies = [pltpu.make_async_copy(a, b, sems.at[n]) for n, (a, b) in enumerate(moves)]
    for copy in copies:
        copy.start()
    for copy in copies:
        copy.wait()
    for at in range(0, width, 256):
        n = min(256, width - at)
        part = amp[:, :, :, :, pl.ds(at, n)].reshape(NX * NZ * rows, n)
        ladder = lax.dot_general(
            part, ints[...], (((0,), (0,)), ((), ())), preferred_element_type=jnp.float32
        )
        quotient = ladder / (vir_ref[...] - occ_ref[pl.ds(lo + at, n), :])
        result[pl.ds(at, n), :] = quotient.astype(result.dtype)
    out = pltpu.make_async_copy(result, out_ref.at[pl.ds(lo, width)], out_sem)
    out.start()
    out.wait()


def fine_place(amp, x, z, offset):
    there = lax.rem(z + offset + NZ, NZ)
    return amp.at[x, :, lax.rem(there, NZF)]


def moves_x_last(pieces, amp, x, z):
    moves = []
    for ref, x_offset in zip(pieces, (0, 1, -1, 2)):
        there = lax.rem(x + x_offset + NX, NX)
        for slot, offset in enumerate((0, 1, -1, 2)):
            moves.append((ref.at[slot], fine_place(amp, there, z, offset)))
    return moves


def moves_z_last(pieces, amp, x, z):
    moves = []
    for ref, offset in zip(pieces, (0, 1, -1, 2)):
        for n in range(NX):
            moves.append((ref.at[n], fine_place(amp, n, z, offset)))
    return moves


def ladder_rows(name, moves_of, lo, pieces, ints, vir, occ, before=None):
    rows, width = pieces[0].shape[2:]
    k_total, vir_here = ints.shape
    occ_here = occ.shape[0]

    def kernel(*refs):
        n = len(pieces)
        skip = 0 if before is None else 1
        ladder_kernel(
            moves_of, lo, (refs[:n], refs[n : n + 3], refs[n + 3 + skip]), refs[n + 4 + skip :]
        )

    any_spec = pl.BlockSpec(memory_space=pl.ANY)
    operands = [*pieces, ints, vir, occ] + ([] if before is None else [before])
    return pl.pallas_call(
        kernel,
        in_specs=[any_spec] * (len(pieces) + 1)
        + [pl.BlockSpec(memory_space=pltpu.VMEM)] * 2
        + [any_spec] * (len(operands) - len(pieces) - 3),
        out_specs=any_spec,
        out_shape=jax.ShapeDtypeStruct((occ_here, vir_here), jnp.bfloat16),
        input_output_aliases={} if before is None else {len(operands) - 1: 0},
        scratch_shapes=[
            pltpu.VMEM((NX, NZC, NZF, rows, width), jnp.bfloat16),
            pltpu.VMEM((k_total, vir_here), jnp.bfloat16),
            pltpu.VMEM((width, vir_here), jnp.bfloat16),
            pltpu.SemaphoreType.DMA((1 + NX * NZF,)),
            pltpu.SemaphoreType.DMA,
        ],
        compiler_params=pltpu.CompilerParams(vmem_limit_bytes=32 * 2**20),
        cost_estimate=pl.CostEstimate(
            flops=2 * width * vir_here * k_total,
            bytes_accessed=2 * (k_total * (width + vir_here) + width * vir_here),
            transcendentals=0,
        ),
        name=name,
    )(*operands)


def shards(amplitudes, amp_mask, integrals, int_mask, owner, occ_energy, vir_energy):
    wide = lax.axis_index("wide")
    narrow = lax.axis_index("narrow")
    src_rows, occ_all = amplitudes.shape
    occ_here = occ_energy.shape[0]
    int_rows, vir_here = integrals.shape
    narrow_count = lax.axis_size("narrow")
    rows = src_rows * narrow_count

    block = lax.all_to_all(
        amplitudes.reshape(src_rows, narrow_count, occ_here),
        "narrow", split_axis=1, concat_axis=0, tiled=True,
    ).reshape(rows, occ_here)
    coarse = share(block, COARSE_Z)
    sources = (wide // NZ) * NZ + jnp.arange(NZC, dtype=jnp.int32) * NZF + wide % NZF
    occ_tiles = occ_here // TILE
    amp_tiles = lax.dynamic_slice_in_dim(amp_mask, narrow * occ_tiles, occ_tiles, 1)
    amp_tiles = jnp.take(amp_tiles, sources * rows // TILE, axis=0)
    amp_wide = jnp.broadcast_to(
        amp_tiles[:, None, :, None], (NZC, 1, occ_tiles, TILE)
    ).reshape(NZC, 1, occ_here)
    coarse = jnp.where(amp_wide == 1, coarse, jnp.zeros((), coarse.dtype))

    vir_tiles_here = vir_here // TILE
    tile_ids = lax.dynamic_slice_in_dim(owner, wide * vir_tiles_here, vir_tiles_here, 0)
    row_tiles = int_rows // TILE
    int_mask_rows = lax.dynamic_slice_in_dim(int_mask, narrow * row_tiles, row_tiles, 0)
    local_mask = jnp.take(int_mask_rows, tile_ids, axis=1)
    local_wide = jnp.broadcast_to(
        local_mask[:, None, :, None], (row_tiles, TILE, vir_tiles_here, TILE)
    ).reshape(int_rows, vir_here)
    int_masked = jnp.where(local_wide == 1, integrals, jnp.zeros((), integrals.dtype))
    int_copies = jnp.broadcast_to(int_masked[None], (narrow_count,) + int_masked.shape)
    int_full = lax.all_to_all(
        int_copies, "narrow", split_axis=0, concat_axis=0, tiled=True
    ).reshape(int_rows * narrow_count, vir_here)

    part_a, part_c = coarse[:, :, :SPLIT], coarse[:, :, SPLIT:]
    fine_a = [from_z(part_a, 2), from_z(part_a, 1), from_z(part_a, -1)]
    x_c = share(part_c, ALONG_X)
    fine_a = jnp.stack([part_a, fine_a[1], fine_a[2], fine_a[0]])
    x_c, fine_a = lax.optimization_barrier((x_c, fine_a))
    a3 = from_x(fine_a, 2)
    a1, a2 = from_x(fine_a, 1), from_x(fine_a, -1)
    c2 = from_z(x_c, 2)
    c0 = from_z(x_c, 1)
    c1 = from_z(x_c, -1)

    vir_here_energy = jnp.take(vir_energy.reshape(-1, TILE), tile_ids, axis=0).reshape(1, vir_here)
    occ = occ_energy.reshape(occ_here, 1)
    first = ladder_rows(
        "ladder_x", moves_x_last, 0, (fine_a, a1, a2, a3), int_full, vir_here_energy, occ
    )
    return ladder_rows(
        "ladder_z", moves_z_last, SPLIT, (x_c, c0, c1, c2), int_full, vir_here_energy, occ, first
    )


def solution(mesh):
    return jax.shard_map(
        shards,
        mesh=mesh,
        in_specs=(
            P(("wide", "narrow"), None),
            P(),
            P("narrow", "wide"),
            P(),
            P(),
            P("narrow"),
            P(),
        ),
        out_specs=P("narrow", "wide"),
        check_vma=False,
    )
```

```python
import jax
import jax.numpy as jnp
from jax import lax
from jax.experimental import pallas as pl
from jax.experimental.pallas import tpu as pltpu
from jax.sharding import PartitionSpec as P

TILE = 64
NX, NZ = 4, 16
NZC, NZF = 4, 4
SPLIT = 512


def from_z(value, offset):
    pairs = [(x * NZ + (z + offset) % NZ, x * NZ + z) for x in range(NX) for z in range(NZ)]
    return lax.ppermute(value, "wide", pairs)


def from_x(value, offset):
    pairs = [(((x + offset) % NX) * NZ + z, x * NZ + z) for x in range(NX) for z in range(NZ)]
    return lax.ppermute(value, "wide", pairs)


def share(value, groups):
    return lax.all_gather(value, "wide", axis_index_groups=groups)


def exchange(value, groups):
    copies = jnp.broadcast_to(value[None], (len(groups[0]),) + value.shape)
    out = lax.all_to_all(
        copies, "wide", split_axis=0, concat_axis=0, axis_index_groups=groups, tiled=True
    )
    return out.reshape((len(groups[0]),) + value.shape)


ALONG_X = [[x * NZ + z for x in range(NX)] for z in range(NZ)]
COARSE_Z = [[x * NZ + c * NZF + f for c in range(NZC)] for x in range(NX) for f in range(NZF)]


def ladder_kernel(moves_of, lo, refs, scratch):
    pieces, (int_ref, vir_ref, occ_ref), out_ref = refs
    amp, result, sems, out_sem = scratch
    rows, width = amp.shape[3:]
    wide = lax.axis_index("wide")
    moves = moves_of(pieces, amp, lax.div(wide, NZ), lax.rem(wide, NZ))
    copies = [pltpu.make_async_copy(a, b, sems.at[n]) for n, (a, b) in enumerate(moves)]
    for copy in copies:
        copy.start()
    for copy in copies:
        copy.wait()
    for at in range(0, width, 256):
        n = min(256, width - at)
        part = amp[:, :, :, :, pl.ds(at, n)].reshape(NX * NZ * rows, n)
        ladder = lax.dot_general(
            part, int_ref[...], (((0,), (0,)), ((), ())), preferred_element_type=jnp.float32
        )
        occ = jnp.broadcast_to(occ_ref[:, pl.ds(lo + at, n)], (8, n)).T[:, :1]
        quotient = ladder / (vir_ref[...] - occ)
        result[pl.ds(at, n), :] = quotient.astype(result.dtype)
    out = pltpu.make_async_copy(result, out_ref.at[pl.ds(lo, width)], out_sem)
    out.start()
    out.wait()


def fine_place(amp, x, z, offset):
    there = lax.rem(z + offset + NZ, NZ)
    return amp.at[x, :, lax.rem(there, NZF)]


def moves_x_last(pieces, amp, x, z):
    moves = []
    ref = pieces[0]
    for there in range(NX):
        for slot, offset in enumerate((0, 1, -1, 2)):
            moves.append((ref.at[there, slot], fine_place(amp, there, z, offset)))
    return moves


def moves_z_last(pieces, amp, x, z):
    moves = []
    half = NX // 2
    for ref, offset, lo in zip(pieces, (0, 1, -1, 2, -2), (0, 0, 0, 0, half)):
        for n in range(ref.shape[0]):
            moves.append((ref.at[n], fine_place(amp, lo + n, z, offset)))
    return moves


def ladder_rows(name, moves_of, lo, pieces, ints, vir, occ, before=None):
    rows, width = pieces[0].shape[-2:]
    k_total, vir_here = ints.shape
    occ_here = occ.shape[1]

    def kernel(*refs):
        n = len(pieces)
        skip = 0 if before is None else 1
        ladder_kernel(
            moves_of, lo, (refs[:n], refs[n : n + 3], refs[n + 3 + skip]), refs[n + 4 + skip :]
        )

    any_spec = pl.BlockSpec(memory_space=pl.ANY)
    operands = [*pieces, ints, vir, occ] + ([] if before is None else [before])
    return pl.pallas_call(
        kernel,
        in_specs=[any_spec] * len(pieces)
        + [pl.BlockSpec(memory_space=pltpu.VMEM)] * 3
        + [any_spec] * (len(operands) - len(pieces) - 3),
        out_specs=any_spec,
        out_shape=jax.ShapeDtypeStruct((occ_here, vir_here), jnp.bfloat16),
        input_output_aliases={} if before is None else {len(operands) - 1: 0},
        scratch_shapes=[
            pltpu.VMEM((NX, NZC, NZF, rows, width), jnp.bfloat16),
            pltpu.VMEM((width, vir_here), jnp.bfloat16),
            pltpu.SemaphoreType.DMA((NX * NZF,)),
            pltpu.SemaphoreType.DMA,
        ],
        compiler_params=pltpu.CompilerParams(vmem_limit_bytes=24 * 2**20),
        cost_estimate=pl.CostEstimate(
            flops=2 * width * vir_here * k_total,
            bytes_accessed=2 * (k_total * (width + vir_here) + width * vir_here),
            transcendentals=0,
        ),
        name=name,
    )(*operands)


def shards(amplitudes, amp_mask, integrals, int_mask, owner, occ_energy, vir_energy):
    wide = lax.axis_index("wide")
    narrow = lax.axis_index("narrow")
    src_rows, occ_all = amplitudes.shape
    occ_here = occ_energy.shape[0]
    int_rows, vir_here = integrals.shape
    narrow_count = lax.axis_size("narrow")
    rows = src_rows * narrow_count

    block = lax.all_to_all(
        amplitudes.reshape(src_rows, narrow_count, occ_here),
        "narrow", split_axis=1, concat_axis=0, tiled=True,
    ).reshape(rows, occ_here)
    coarse = share(block, COARSE_Z)
    sources = (wide // NZ) * NZ + jnp.arange(NZC, dtype=jnp.int32) * NZF + wide % NZF
    occ_tiles = occ_here // TILE
    amp_tiles = lax.dynamic_slice_in_dim(amp_mask, narrow * occ_tiles, occ_tiles, 1)
    amp_tiles = jnp.take(amp_tiles, sources * rows // TILE, axis=0)
    amp_wide = jnp.broadcast_to(
        amp_tiles[:, None, :, None], (NZC, 1, occ_tiles, TILE)
    ).reshape(NZC, 1, occ_here)
    coarse = jnp.where(amp_wide == 1, coarse, jnp.zeros((), coarse.dtype))

    vir_tiles_here = vir_here // TILE
    tile_ids = lax.dynamic_slice_in_dim(owner, wide * vir_tiles_here, vir_tiles_here, 0)
    row_tiles = int_rows // TILE
    int_mask_rows = lax.dynamic_slice_in_dim(int_mask, narrow * row_tiles, row_tiles, 0)
    local_mask = jnp.take(int_mask_rows, tile_ids, axis=1)
    local_wide = jnp.broadcast_to(
        local_mask[:, None, :, None], (row_tiles, TILE, vir_tiles_here, TILE)
    ).reshape(int_rows, vir_here)
    int_masked = jnp.where(local_wide == 1, integrals, jnp.zeros((), integrals.dtype))
    int_copies = jnp.broadcast_to(int_masked[None], (narrow_count,) + int_masked.shape)
    int_full = lax.all_to_all(
        int_copies, "narrow", split_axis=0, concat_axis=0, tiled=True
    ).reshape(int_rows * narrow_count, vir_here)

    part_a, part_c = coarse[:, :, :SPLIT], coarse[:, :, SPLIT:]
    fine_a = [from_z(part_a, 2), from_z(part_a, 1), from_z(part_a, -1)]
    x_c = share(part_c, ALONG_X)
    fine_a = jnp.stack([part_a, fine_a[1], fine_a[2], fine_a[0]])
    x_c, fine_a, int_full = lax.optimization_barrier((x_c, fine_a, int_full))
    whole_a = exchange(fine_a, ALONG_X)
    half = NX // 2
    c2 = from_z(x_c[:half], 2)
    c3 = from_z(x_c[half:], -2)
    c0 = from_z(x_c, 1)
    c1 = from_z(x_c, -1)

    vir_here_energy = jnp.take(vir_energy.reshape(-1, TILE), tile_ids, axis=0).reshape(1, vir_here)
    occ = occ_energy.reshape(1, occ_here)
    first = ladder_rows(
        "ladder_x", moves_x_last, 0, (whole_a,), int_full, vir_here_energy, occ
    )
    return ladder_rows(
        "ladder_z", moves_z_last, SPLIT, (x_c, c0, c1, c2, c3), int_full, vir_here_energy, occ, first
    )


def solution(mesh):
    return jax.shard_map(
        shards,
        mesh=mesh,
        in_specs=(
            P(("wide", "narrow"), None),
            P(),
            P("narrow", "wide"),
            P(),
            P(),
            P("narrow"),
            P(),
        ),
        out_specs=P("narrow", "wide"),
        check_vma=False,
    )
```

```python
import jax
import jax.numpy as jnp
from jax import lax
from jax.experimental import pallas as pl
from jax.experimental.pallas import tpu as pltpu
from jax.sharding import PartitionSpec as P


TILE = 64
NX, NZ = 4, 16
NZC, NZF = 4, 4
SPLIT = 512


def from_z(value, offset):
    pairs = [(x * NZ + (z + offset) % NZ, x * NZ + z) for x in range(NX) for z in range(NZ)]
    return lax.ppermute(value, "wide", pairs)


def share(value, groups):
    return lax.all_gather(value, "wide", axis_index_groups=groups)


def exchange(value, groups):
    copies = jnp.broadcast_to(value[None], (len(groups[0]),) + value.shape)
    out = lax.all_to_all(
        copies, "wide", split_axis=0, concat_axis=0, axis_index_groups=groups, tiled=True
    )
    return out.reshape((len(groups[0]),) + value.shape)


ALONG_X = [[x * NZ + z for x in range(NX)] for z in range(NZ)]
COARSE_Z = [[x * NZ + c * NZF + f for c in range(NZC)] for x in range(NX) for f in range(NZF)]


def ladder_kernel(moves_of, lo, refs, scratch):
    pieces, (int_ref, vir_ref, occ_ref), out_ref = refs
    amp, result, sems, out_sem = scratch
    rows, width = amp.shape[3:]
    wide = lax.axis_index("wide")
    moves = moves_of(pieces, amp, lax.div(wide, NZ), lax.rem(wide, NZ))
    copies = [pltpu.make_async_copy(a, b, sems.at[n]) for n, (a, b) in enumerate(moves)]
    for copy in copies:
        copy.start()
    for copy in copies:
        copy.wait()
    for at in range(0, width, 256):
        n = min(256, width - at)
        part = amp[:, :, :, :, pl.ds(at, n)].reshape(NX * NZ * rows, n)
        ladder = lax.dot_general(
            part, int_ref[...], (((0,), (0,)), ((), ())), preferred_element_type=jnp.float32
        )
        occ = jnp.broadcast_to(occ_ref[:, pl.ds(lo + at, n)], (8, n)).T[:, :1]
        quotient = ladder / (vir_ref[...] - occ)
        result[pl.ds(at, n), :] = quotient.astype(result.dtype)
    out = pltpu.make_async_copy(result, out_ref.at[pl.ds(lo, width)], out_sem)
    out.start()
    out.wait()


def fine_place(amp, x, z, offset):
    there = lax.rem(z + offset + NZ, NZ)
    return amp.at[x, :, lax.rem(there, NZF)]


def moves_x_last(pieces, amp, x, z):
    moves = []
    ref = pieces[0]
    for there in range(NX):
        for slot, offset in enumerate((0, 1, -1, 2)):
            moves.append((ref.at[there, slot], fine_place(amp, there, z, offset)))
    return moves


def moves_z_last(pieces, amp, x, z):
    moves = []
    half = NX // 2
    for ref, offset, lo in zip(pieces, (0, 1, -1, 2, -2), (0, 0, 0, 0, half)):
        for n in range(ref.shape[0]):
            moves.append((ref.at[n], fine_place(amp, lo + n, z, offset)))
    return moves


def ladder_rows(moves_of, lo, pieces, ints, vir, occ, before=None):
    rows, width = pieces[0].shape[-2:]
    k_total, vir_here = ints.shape
    occ_here = occ.shape[1]

    def kernel(*refs):
        n = len(pieces)
        skip = 0 if before is None else 1
        ladder_kernel(
            moves_of, lo, (refs[:n], refs[n : n + 3], refs[n + 3 + skip]), refs[n + 4 + skip :]
        )

    any_spec = pl.BlockSpec(memory_space=pl.ANY)
    operands = [*pieces, ints, vir, occ] + ([] if before is None else [before])
    return pl.pallas_call(
        kernel,
        in_specs=[any_spec] * len(pieces)
        + [pl.BlockSpec(memory_space=pltpu.VMEM)] * 3
        + [any_spec] * (len(operands) - len(pieces) - 3),
        out_specs=any_spec,
        out_shape=jax.ShapeDtypeStruct((occ_here, vir_here), jnp.bfloat16),
        input_output_aliases={} if before is None else {len(operands) - 1: 0},
        scratch_shapes=[
            pltpu.VMEM((NX, NZC, NZF, rows, width), jnp.bfloat16),
            pltpu.VMEM((width, vir_here), jnp.bfloat16),
            pltpu.SemaphoreType.DMA((NX * NZF,)),
            pltpu.SemaphoreType.DMA,
        ],
        compiler_params=pltpu.CompilerParams(vmem_limit_bytes=24 * 2**20),
        cost_estimate=pl.CostEstimate(
            flops=2 * width * vir_here * k_total,
            bytes_accessed=2 * (k_total * (width + vir_here) + width * vir_here),
            transcendentals=0,
        ),
    )(*operands)


def shards(amplitudes, amp_mask, integrals, int_mask, owner, occ_energy, vir_energy):
    wide = lax.axis_index("wide")
    narrow = lax.axis_index("narrow")
    src_rows, _ = amplitudes.shape
    occ_here = occ_energy.shape[0]
    int_rows, vir_here = integrals.shape
    narrow_count = lax.axis_size("narrow")
    rows = src_rows * narrow_count

    block = lax.all_to_all(
        amplitudes.reshape(src_rows, narrow_count, occ_here),
        "narrow", split_axis=1, concat_axis=0, tiled=True,
    ).reshape(rows, occ_here)
    coarse = share(block, COARSE_Z)
    sources = (wide // NZ) * NZ + jnp.arange(NZC, dtype=jnp.int32) * NZF + wide % NZF
    occ_tiles = occ_here // TILE
    amp_tiles = lax.dynamic_slice_in_dim(amp_mask, narrow * occ_tiles, occ_tiles, 1)
    amp_tiles = jnp.take(amp_tiles, sources * rows // TILE, axis=0)
    amp_wide = jnp.broadcast_to(
        amp_tiles[:, None, :, None], (NZC, 1, occ_tiles, TILE)
    ).reshape(NZC, 1, occ_here)
    coarse = jnp.where(amp_wide == 1, coarse, jnp.zeros((), coarse.dtype))

    vir_tiles_here = vir_here // TILE
    tile_ids = lax.dynamic_slice_in_dim(owner, wide * vir_tiles_here, vir_tiles_here, 0)
    row_tiles = int_rows // TILE
    int_mask_rows = lax.dynamic_slice_in_dim(int_mask, narrow * row_tiles, row_tiles, 0)
    local_mask = jnp.take(int_mask_rows, tile_ids, axis=1)
    local_wide = jnp.broadcast_to(
        local_mask[:, None, :, None], (row_tiles, TILE, vir_tiles_here, TILE)
    ).reshape(int_rows, vir_here)
    int_masked = jnp.where(local_wide == 1, integrals, jnp.zeros((), integrals.dtype))
    int_copies = jnp.broadcast_to(int_masked[None], (narrow_count,) + int_masked.shape)
    int_full = lax.all_to_all(
        int_copies, "narrow", split_axis=0, concat_axis=0, tiled=True
    ).reshape(int_rows * narrow_count, vir_here)

    part_a, part_c = coarse[:, :, :SPLIT], coarse[:, :, SPLIT:]
    fine_a = [from_z(part_a, 2), from_z(part_a, 1), from_z(part_a, -1)]
    x_c = share(part_c, ALONG_X)
    fine_a = jnp.stack([part_a, fine_a[1], fine_a[2], fine_a[0]])
    x_c, fine_a, int_full = lax.optimization_barrier((x_c, fine_a, int_full))
    whole_a = exchange(fine_a, ALONG_X)
    half = NX // 2
    c2 = from_z(x_c[:half], 2)
    c3 = from_z(x_c[half:], -2)
    c0 = from_z(x_c, 1)
    c1 = from_z(x_c, -1)

    vir_here_energy = jnp.take(vir_energy.reshape(-1, TILE), tile_ids, axis=0).reshape(1, vir_here)

    occ = occ_energy.reshape(1, occ_here)
    first = ladder_rows(moves_x_last, 0, (whole_a,), int_full, vir_here_energy, occ)
    return ladder_rows(
        moves_z_last, SPLIT, (x_c, c0, c1, c2, c3), int_full, vir_here_energy, occ, first
    )


def solution(mesh):
    return jax.shard_map(
        shards,
        mesh=mesh,
        in_specs=(
            P(("wide", "narrow"), None),
            P(),
            P("narrow", "wide"),
            P(),
            P(),
            P("narrow"),
            P(),
        ),
        out_specs=P("narrow", "wide"),
        check_vma=False,
    )
```
